32 devices in a mesh: groups: 2 (over y), sub: 4 (over z), clus: 2 (over x), rep: 2 (over core).
Axes of the slice: x: 2, y: 2, z: 4, core: 2. Of those that a mesh axis runs over, the one named last changes fastest.
Arguments:
- dual_ops: float32 [4, 4, 1536, 1536], P(('groups', 'clus'), 'sub'), parts along dimension 0, as said below
- block_index: int32 [4, 4, 12], P(('groups', 'clus'), 'sub'), parts along dimension 0, may hold values from 0 to 11, as said below
- live_blocks: int32 [4, 4], P(('groups', 'clus'), 'sub'), parts along dimension 0, may hold values from 6 to 12
- loads: float32 [4, 1536, 128], P(('groups', 'clus'), 'sub', 'rep'), parts along dimension 0, may hold values from -6 to 6
- coupling: float32 [4, 1536, 128], P(('groups', 'clus'), 'sub'), parts along dimension 0, may hold values from -0.125 to 0.125
- neighbours: int32 [4, 2], P(('groups', 'clus')), parts along dimension 0, may hold values from 0 to 1, as said below
- bound_len: int32 [4, 2], P(('groups', 'clus')), parts along dimension 0, may hold values from 32 to 128
Outputs:
- multipliers: float32 [4, 1536, 128], P(('groups', 'clus'), 'sub', 'rep'), parts along dimension 0
The draws below stay inside these ranges and needn't reach their ends.
There are 2 independent parts, one for each index of `groups`. The reference program is written for one: setup_inputs(seed, part) draws one part's arguments, and reference() takes and returns one part's arrays. A program takes and returns all parts, laid end to end along the dimension named above; each array names one. Nothing has to cross between parts.
Inputs may be any that keep to these rules, and one draw needn't show every extreme that they name: The entries of block_index[c, s] are distinct, the first 3 of them are 3 * s to 3 * s + 2, and among the others at most 3 lie in the range 3 * t to 3 * t + 2 of any one t; some t holds exactly 3 of them. neighbours[c, j] may be c itself, a periodic boundary of the cluster. Each dual_ops[c, s] is symmetric positive definite with diagonal entries of 1 or more.
All inputs are finite; a program needn't handle non-finite values.
Results may differ from the reference program's by a relative error of at most 0.0001.
Values sent between devices are 32-bit elements; how exact they have to be, the bound alone decides.
No kernel may reach another device: no remote copies, remote signals or barrier semaphores. Data moves between devices by JAX's collectives and lax.ppermute only.
A program may use at most 128 MiB of HBM per device.

```python
import jax
import jax.numpy as jnp
from jax import lax

MB = 12
BLK = 128
K = 128
NB_DEV = 3
BR = 128
NNB = 2
CYCLES = 2
CHEB = 3
NSUBS = 4
NCLUS = 2
NROWS = 1536


coupling_spread = 0.4


def draw_dual_ops(key, part):
    order = MB * BLK
    base_key = jax.random.fold_in(key, 23)

    def single(sub_key):
        diag_key, off_key = jax.random.split(sub_key)
        diag_vals = jax.random.uniform(diag_key, (order,), jnp.float32, 1.0, 3.0)
        normal_draw = jax.random.normal(off_key, (order, order), jnp.float32)
        wigner = (normal_draw + normal_draw.T) / jnp.sqrt(2.0 * order)
        wigner = wigner * (1.0 - jnp.eye(order, dtype=jnp.float32))
        return coupling_spread * wigner + jnp.diag(diag_vals)
    sub_keys = jax.random.split(base_key, NCLUS * NSUBS)
    return lax.map(single, sub_keys).reshape(NCLUS, NSUBS, order, order)


def draw_block_index(key, part):
    peers = NSUBS - 1
    foreign = MB - NB_DEV

    def single(sub_key, owner):
        perm_key, row_key = jax.random.split(sub_key)
        shuffled = jax.random.permutation(perm_key, peers).astype(jnp.int32)
        others = jnp.where(shuffled >= owner, shuffled + 1, shuffled)
        starts = jax.random.randint(row_key, (peers,), 0, NB_DEV).astype(jnp.int32)
        slots = jnp.arange(foreign, dtype=jnp.int32)
        turn = slots % peers
        rounds = slots // peers
        far_owner = others[turn]
        far_row = (starts[turn] + rounds) % NB_DEV
        owned_ids = owner * NB_DEV + jnp.arange(NB_DEV, dtype=jnp.int32)
        return jnp.concatenate([owned_ids, far_owner * NB_DEV + far_row])
    key_list = jax.random.split(jax.random.fold_in(key, 11), NCLUS * NSUBS)
    owners = jnp.tile(jnp.arange(NSUBS, dtype=jnp.int32), NCLUS)
    return jax.vmap(single)(key_list, owners).reshape(NCLUS, NSUBS, MB)


def draw_neighbours(key, part):
    drawn = jax.random.randint(jax.random.fold_in(key, 31), (NCLUS, NNB), 0, NCLUS)
    return drawn.astype(jnp.int32)


def plant(array, stream_key, smallest, top_value):
    index_at = [jax.random.randint(jax.random.fold_in(stream_key, axis), (), 0, length) for axis, length in enumerate(array.shape)]
    longest = array.shape.index(max(array.shape))
    neighbour = index_at[:longest] + [(index_at[longest] + 1) % array.shape[longest]] + index_at[longest + 1:]
    return array.at[tuple(index_at)].set(smallest).at[tuple(neighbour)].set(top_value)


def steps_of(rng, dims, shards, low, high):
    level, own = 1.0, jax.random.fold_in(rng, 6)
    for dim, parts in shards:
        heights = jnp.exp(jax.random.uniform(jax.random.fold_in(own, dim), (parts,), jnp.float32, low / len(shards), high / len(shards)))
        level = level * jnp.repeat(heights, dims[dim] // parts).reshape([-1 if axis == dim else 1 for axis in range(len(dims))])
    return level


def scatter_about(rng, extent, spread, most, cuts=(), kind=jnp.bfloat16):
    values = spread * jax.random.normal(rng, extent, jnp.float32)
    if cuts:
        values = values * steps_of(rng, extent, cuts, -0.22, 0.18)
    return jnp.clip(values, -most, most).astype(kind)


def setup_inputs(seed: int = 0, part: int = 0) -> dict:
    streams_of = jax.random.split(jax.random.key(seed), 8)
    part_keys = jax.random.split(jax.random.fold_in(streams_of[7], part), 8)
    return {
        "dual_ops": draw_dual_ops(jax.random.fold_in(jax.random.fold_in(streams_of[7], part), 71), part),
        "block_index": draw_block_index(jax.random.fold_in(jax.random.fold_in(streams_of[7], part), 71), part),
        "live_blocks": plant(jax.random.randint(part_keys[2], (NCLUS, NSUBS), MB // 2, MB + 1), jax.random.fold_in(part_keys[2], 1), MB // 2, MB).astype(jnp.int32),
        "loads": scatter_about(part_keys[3], (NCLUS, NROWS, K), 1.0, 6.0, ((0, 2), (1, 4), (2, 2)), jnp.float32),
        "coupling": scatter_about(part_keys[4], (NCLUS, NROWS, BR), (BR * 16) ** -0.5, 0.125, ((0, 2), (1, 4)), jnp.float32),
        "neighbours": draw_neighbours(jax.random.fold_in(jax.random.fold_in(streams_of[7], part), 71), part),
        "bound_len": plant(jax.random.randint(part_keys[6], (NCLUS, NNB), BR // 4, BR + 1), jax.random.fold_in(part_keys[6], 1), BR // 4, BR).astype(jnp.int32),
    }


highest = lax.Precision.HIGHEST
theta = 1.0
delta = 0.8


def pick_blocks(table, indices):
    return table[indices]


def add_blocks(table, indices, values):
    return table.at[indices].add(values)


def add_diagonal(indices, values, template):
    return template.at[indices].add(values)


def reference(dual_ops, block_index, live_blocks, loads, coupling, neighbours, bound_len):
    clusters = dual_ops.shape[0]
    subdomains = dual_ops.shape[1]
    order = dual_ops.shape[2]
    blocks = block_index.shape[2]
    columns = loads.shape[2]
    total_blocks = loads.shape[1] // BLK
    live = (jnp.arange(blocks, dtype=jnp.int32)[None, None, :] < live_blocks[:, :, None]).astype(jnp.float32)
    diag_vals = jnp.diagonal(dual_ops, axis1=2, axis2=3).reshape(clusters, subdomains, blocks, BLK) * live[:, :, :, None]
    template = jnp.zeros((total_blocks, BLK), jnp.float32)
    diag_sum = jax.vmap(lambda indices, values: add_diagonal(indices, values, template))(
        block_index.reshape(clusters, subdomains * blocks), diag_vals.reshape(clusters, subdomains * blocks, BLK))
    inverse = (1.0 / diag_sum)[:, :, :, None]

    def apply_operator(vector):
        def per_subdomain(totals, index):
            operators = lax.dynamic_index_in_dim(dual_ops, index, 1, keepdims=False)
            chosen = lax.dynamic_index_in_dim(block_index, index, 1, keepdims=False)
            weights = lax.dynamic_index_in_dim(live, index, 1, keepdims=False)
            gathered = jax.vmap(pick_blocks)(vector, chosen) * weights[:, :, None, None]
            product = jnp.einsum("cij,cjk->cik", operators, gathered.reshape(clusters, order, columns), precision=highest)
            product = product.reshape(clusters, blocks, BLK, columns) * weights[:, :, None, None]
            return jax.vmap(add_blocks)(totals, chosen, product), None
        totals, ignored = lax.scan(per_subdomain, jnp.zeros_like(vector), jnp.arange(subdomains, dtype=jnp.int32))
        return totals

    load_rows = loads.reshape(clusters, total_blocks, BLK, columns)
    multipliers = jnp.zeros_like(load_rows)
    sigma = theta / delta
    row_mask = (jnp.arange(coupling.shape[2], dtype=jnp.int32)[None, None, :] < bound_len[:, :, None]).astype(jnp.float32)
    for cycle_index in range(CYCLES):
        if cycle_index == 0:
            residual = load_rows
        else:
            residual = load_rows - apply_operator(multipliers)
        update = inverse * residual / theta
        ratio_prev = 1.0 / sigma
        for sweep_index in range(CHEB):
            multipliers = multipliers + update
            if sweep_index + 1 < CHEB:
                residual = residual - apply_operator(update)
                ratio_next = 1.0 / (2.0 * sigma - ratio_prev)
                update = ratio_next * ratio_prev * update + (2.0 * ratio_next / delta) * inverse * residual
                ratio_prev = ratio_next
        flattened = multipliers.reshape(clusters, total_blocks * BLK, columns)
        responses = jnp.einsum("crb,crk->cbk", coupling, flattened, precision=highest)
        picked = responses[neighbours]
        incoming = jnp.sum(row_mask[:, :, :, None] * picked, axis=1)
        correction = jnp.einsum("crb,cbk->crk", coupling, incoming, precision=highest)
        multipliers = multipliers + inverse * correction.reshape(clusters, total_blocks, BLK, columns)
    return multipliers.reshape(clusters, total_blocks * BLK, columns)
```

```python
import functools

import jax
import jax.numpy as jnp
from jax import lax
from jax.experimental import pallas as pl
from jax.experimental.pallas import tpu as pltpu
from jax.sharding import PartitionSpec as P

BLK = 128
CYCLES = 2
CHEB = 3

highest = lax.Precision.HIGHEST
theta = 1.0
delta = 0.8

VMEM = pl.BlockSpec(memory_space=pltpu.VMEM)
SMEM = pl.BlockSpec(memory_space=pltpu.SMEM)
ANY = pl.BlockSpec(memory_space=pl.ANY)


def dot32(left, right):
    return jnp.dot(left, right, preferred_element_type=jnp.float32)


def halves(value):
    high = value.astype(jnp.bfloat16)
    return high, (value - high.astype(jnp.float32)).astype(jnp.bfloat16)


def diagonal_kernel(blocks, order, alive, operator, diag, tiles, sems):
    copies = []
    for p in range(blocks):
        at = pl.ds(pl.multiple_of(order[p] * BLK, BLK), BLK)
        copies.append(pltpu.make_async_copy(operator.at[at, at], tiles.at[p], sems.at[p]))
        copies[-1].start()
    rows = lax.broadcasted_iota(jnp.int32, (BLK, BLK), 0)
    cols = lax.broadcasted_iota(jnp.int32, (BLK, BLK), 1)
    for p in range(blocks):
        copies[p].wait()
        kept = jnp.where(rows == cols, tiles[p], 0.0)
        diag[p : p + 1, :] = jnp.sum(kept, axis=0, keepdims=True) * alive[p]


def diagonal(order, alive, operator, blocks):
    return pl.pallas_call(
        functools.partial(diagonal_kernel, blocks),
        out_shape=jax.ShapeDtypeStruct((blocks, BLK), jnp.float32),
        in_specs=[SMEM, SMEM, ANY],
        out_specs=VMEM,
        scratch_shapes=[
            pltpu.VMEM((blocks, BLK, BLK), jnp.float32),
            pltpu.SemaphoreType.DMA((blocks,)),
        ],
        compiler_params=pltpu.CompilerParams(vmem_limit_bytes=8 << 20),
        cost_estimate=pl.CostEstimate(
            flops=blocks * BLK * BLK, bytes_accessed=4 * blocks * BLK * BLK, transcendentals=0
        ),
        name="diagonal",
    )(order, alive, operator)


def prepare_kernel(blocks, order, alive, operator, high, low):
    def row_block(p, carry):
        source = pl.ds(pl.multiple_of(order[p] * BLK, BLK), BLK)
        target = pl.ds(pl.multiple_of(p * BLK, BLK), BLK)
        for q in range(blocks):
            across = pl.ds(pl.multiple_of(order[q] * BLK, BLK), BLK)
            tile = operator[source, across] * (alive[p] * alive[q])
            high_part, low_part = halves(tile)
            high[target, q * BLK : (q + 1) * BLK] = high_part
            low[target, q * BLK : (q + 1) * BLK] = low_part
        return carry

    lax.fori_loop(0, blocks, row_block, 0)


def prepare(order, alive, operator, blocks):
    size = blocks * BLK
    shape = jax.ShapeDtypeStruct((size, size), jnp.bfloat16)
    return pl.pallas_call(
        functools.partial(prepare_kernel, blocks),
        out_shape=(shape, shape),
        in_specs=[SMEM, SMEM, VMEM],
        out_specs=[VMEM, VMEM],
        compiler_params=pltpu.CompilerParams(vmem_limit_bytes=8 << 20),
        cost_estimate=pl.CostEstimate(
            flops=2 * size * size, bytes_accessed=8 * size * size, transcendentals=0
        ),
        name="prepare",
    )(order, alive, operator)


def product_kernel(counts, columns, scaled, *refs):
    high, low = refs[:2]
    refs = refs[2:]
    scale = None
    if scaled:
        scale, refs = refs[0], refs[1:]
    values, outs, packed = refs[: len(counts)], refs[len(counts) : 2 * len(counts)], refs[-1]
    position = 0
    for count, value in zip(counts, values):
        for k in range(count):
            part = value[k]
            if scaled:
                part = part * scale[position : position + 1, :]
            high_part, low_part = halves(part)
            across = slice(position * BLK, (position + 1) * BLK)
            packed[:columns, across] = high_part
            packed[columns:, across] = low_part
            position += 1
    position = 0
    for count, out in zip(counts, outs):
        across = slice(position * BLK, (position + count) * BLK)
        both = dot32(packed[...], high[:, across])
        total = both[:columns] + both[columns:] + dot32(packed[:columns, :], low[:, across])
        for k in range(count):
            out[k] = total[:, k * BLK : (k + 1) * BLK]
        position += count


def product(high, low, values, scale=None):
    counts = [value.shape[0] for value in values]
    columns = values[0].shape[1]
    size = high.shape[0]
    scaled = scale is not None
    return pl.pallas_call(
        functools.partial(product_kernel, counts, columns, scaled),
        out_shape=tuple(jax.ShapeDtypeStruct(value.shape, jnp.float32) for value in values),
        in_specs=[VMEM] * (2 + scaled + len(counts)),
        out_specs=[VMEM] * len(counts),
        scratch_shapes=[pltpu.VMEM((2 * columns, size), jnp.bfloat16)],
        compiler_params=pltpu.CompilerParams(vmem_limit_bytes=16 << 20),
        cost_estimate=pl.CostEstimate(
            flops=6 * size * size * columns, bytes_accessed=4 * size * size, transcendentals=0
        ),
        name="product",
    )(high, low, *([scale] if scaled else []), *values)


def partner(value, axis, step):
    count = lax.axis_size(axis)
    return lax.ppermute(value, axis, [(i, i ^ step) for i in range(count)])


class Dense:
    def __init__(self, operator, block_index, live_count, owned):
        self.count = lax.axis_size("sub")
        self.owned = owned
        blocks = block_index.shape[0]
        me = lax.axis_index("sub")
        slots = lax.iota(jnp.int32, blocks)
        wanted = (me ^ (slots // owned)) * owned + slots % owned
        hit = (wanted[:, None] == block_index[None, :]).astype(jnp.int32)
        order = jnp.sum(hit * slots[None, :], axis=1)
        alive = (order < live_count).astype(jnp.float32)
        diag = diagonal(order, alive, operator, blocks).reshape(self.count, owned, BLK)
        parts = [diag] + [partner(diag, "sub", d) for d in range(1, self.count)]
        rows = []
        for e in range(self.count):
            rows.append(sum(parts[d][d ^ e] for d in range(self.count)))
        self.inverse_all = 1.0 / jnp.concatenate(rows, axis=0)
        self.high, self.low = prepare(order, alive, operator, blocks)

    def inverse(self):
        return self.inverse_all[: self.owned]

    def spread(self, vector):
        return [vector] + [partner(vector, "sub", d) for d in range(1, self.count)]

    def collect(self, products):
        arrived = [partner(products[d], "sub", d) for d in range(1, self.count)]
        return sum(arrived, products[0])

    def first(self, loads):
        return self.collect(product(self.high, self.low, self.spread(loads), self.inverse_all))

    def apply(self, vector):
        return self.collect(product(self.high, self.low, self.spread(vector)))

    def total(self, value):
        for_sum = [partner(value, "sub", d) for d in range(1, self.count)]
        return sum(for_sum, value)


class Sparse:
    def __init__(self, operator, block_index, live_count, owned):
        blocks = block_index.shape[0]
        subdomains = lax.axis_size("sub")
        self.owned = owned
        self.subdomains = subdomains
        order = lax.iota(jnp.int32, blocks)
        alive = (order < live_count).astype(jnp.float32)
        total_blocks = owned * subdomains
        diag = diagonal(order, alive, operator, blocks)
        picker = (block_index[:, None] == lax.iota(jnp.int32, total_blocks)[None, :]).astype(
            jnp.float32
        )
        diag_term = jnp.dot(picker.T, diag, precision=highest)
        diag_sum = lax.psum_scatter(diag_term, "sub", scatter_dimension=0, tiled=True)
        self.inverse_own = 1.0 / diag_sum
        self.high, self.low = prepare(order, alive, operator, blocks)
        foreign = blocks - owned
        capacity = (foreign + subdomains - 2) // (subdomains - 1)
        self.capacity = capacity
        total_slots = subdomains * capacity
        far_ids = block_index[owned:]
        far_owner = far_ids // owned
        far_row = far_ids % owned
        positions = lax.iota(jnp.int32, foreign)
        earlier = (
            (far_owner[:, None] == far_owner[None, :]) & (positions[None, :] < positions[:, None])
        ).astype(jnp.int32)
        slot = far_owner * capacity + jnp.sum(earlier, axis=1)
        slot_hit = (slot[:, None] == lax.iota(jnp.int32, total_slots)[None, :]).astype(jnp.int32)
        self.slot_pick = slot_hit.astype(jnp.float32)
        filled = jnp.sum(slot_hit, axis=0)
        wanted = jnp.where(filled > 0, jnp.sum(slot_hit * far_row[:, None], axis=0), -1)
        asked = self.exchange(wanted)
        self.reply_pick = (asked[:, None] == lax.iota(jnp.int32, owned)[None, :]).astype(
            jnp.float32
        )

    def exchange(self, value):
        shape = value.shape
        value = value.reshape((self.subdomains, self.capacity) + shape[1:])
        value = lax.all_to_all(value, "sub", split_axis=0, concat_axis=0, tiled=True)
        return value.reshape(shape)

    def pick(self, table, value):
        return jnp.einsum("pq,qcr->pcr", table, value, precision=highest)

    def inverse(self):
        return self.inverse_own

    def first(self, loads):
        return self.apply(loads * self.inverse_own[:, None, :])

    def apply(self, vector):
        fetched = self.exchange(self.pick(self.reply_pick, vector))
        far = self.pick(self.slot_pick, fetched)
        (result,) = product(self.high, self.low, [jnp.concatenate([vector, far], axis=0)])
        sending = self.pick(self.slot_pick.T, result[self.owned :])
        returned = self.exchange(sending)
        return result[: self.owned] + self.pick(self.reply_pick.T, returned)

    def total(self, value):
        return lax.psum(value, "sub")


def local(dual_ops, block_index, live_blocks, loads, coupling, neighbours, bound_len):
    operator = dual_ops[0, 0]
    blocks = block_index.shape[2]
    owned = loads.shape[1] // BLK
    columns = loads.shape[2]
    subdomains = lax.axis_size("sub")
    clusters = lax.axis_size("clus")
    everyone = blocks == owned * subdomains and subdomains & (subdomains - 1) == 0
    plan = (Dense if everyone else Sparse)(operator, block_index[0, 0], live_blocks[0, 0], owned)
    loads_t = jnp.swapaxes(loads[0].reshape(owned, BLK, columns), 1, 2)
    maps = coupling[0].reshape(owned, BLK, coupling.shape[2])
    inverse = plan.inverse()[:, None, :]
    here = lax.axis_index("clus")
    row_mask = (lax.iota(jnp.int32, coupling.shape[2])[None, :] < bound_len[0][:, None]).astype(
        jnp.float32
    )
    weights = []
    for e in range(clusters):
        chosen = (neighbours[0] == (here + e) % clusters).astype(jnp.float32)
        weights.append(jnp.sum(chosen[:, None] * row_mask, axis=0))
    sigma = theta / delta
    multipliers = jnp.zeros_like(loads_t)
    for cycle_index in range(CYCLES):
        if cycle_index == 0:
            residual = loads_t
        else:
            residual = loads_t - plan.apply(multipliers)
        update = inverse * residual / theta
        ratio_prev = 1.0 / sigma
        for sweep_index in range(CHEB):
            multipliers = multipliers + update
            if sweep_index + 1 < CHEB:
                if cycle_index == 0 and sweep_index == 0:
                    applied = plan.first(loads_t) / theta
                else:
                    applied = plan.apply(update)
                residual = residual - applied
                ratio_next = 1.0 / (2.0 * sigma - ratio_prev)
                update = (
                    ratio_next * ratio_prev * update + 2.0 * ratio_next / delta * inverse * residual
                )
                ratio_prev = ratio_next
        partial_sum = jnp.einsum("rkn,rnb->kb", multipliers, maps, precision=highest)
        responses = plan.total(partial_sum)
        incoming = weights[0] * responses
        for e in range(1, clusters):
            arrived = lax.ppermute(
                responses, "clus", [((i + e) % clusters, i) for i in range(clusters)]
            )
            incoming = incoming + weights[e] * arrived
        correction = jnp.einsum("kb,rnb->rkn", incoming, maps, precision=highest)
        multipliers = multipliers + inverse * correction
    return jnp.swapaxes(multipliers, 1, 2).reshape(1, owned * BLK, columns)


def solution(mesh):
    placed = (
        P(("groups", "clus"), "sub", None, None),
        P(("groups", "clus"), "sub", None),
        P(("groups", "clus"), "sub"),
        P(("groups", "clus"), "sub", "rep"),
        P(("groups", "clus"), "sub", None),
        P(("groups", "clus"), None),
        P(("groups", "clus"), None),
    )
    return jax.shard_map(
        local,
        mesh=mesh,
        in_specs=placed,
        out_specs=P(("groups", "clus"), "sub", "rep"),
        check_vma=False,
    )
```

```python
import functools

import jax
import jax.numpy as jnp
from jax import lax
from jax.experimental import pallas as pl
from jax.experimental.pallas import tpu as pltpu
from jax.sharding import PartitionSpec as P

BLK = 128
CYCLES = 2
CHEB = 3

highest = lax.Precision.HIGHEST
theta = 1.0
delta = 0.8

VMEM = pl.BlockSpec(memory_space=pltpu.VMEM)
SMEM = pl.BlockSpec(memory_space=pltpu.SMEM)
ANY = pl.BlockSpec(memory_space=pl.ANY)


def dot32(left, right):
    return jnp.dot(left, right, preferred_element_type=jnp.float32)


def dot32_t(left, right):
    return lax.dot_general(
        left, right, (((1,), (1,)), ((), ())), preferred_element_type=jnp.float32
    )


def halves(value):
    high = value.astype(jnp.bfloat16)
    return high, (value - high.astype(jnp.float32)).astype(jnp.bfloat16)


def three_products(dot, packed, high, low):
    count = packed.shape[0] // 2
    both = dot(packed, high)
    return both[:count] + both[count:] + dot(packed[:count], low)


def pinned(value):
    return pltpu.with_memory_space_constraint(value, pltpu.VMEM)


def place_of(position, owned, block_index):
    if owned is None:
        return 0, position
    block = block_index[0, 0, position]
    return lax.div(block, owned) ^ lax.axis_index("sub"), lax.rem(block, owned)


def aligned(block):
    return pl.ds(pl.multiple_of(block * BLK, BLK), BLK)


def diagonal_kernel(blocks, owned, reps, block_index, live_blocks, operator, *refs):
    if owned:
        coupling, diag, part, tiles, lines, sems, part_sems = refs
    else:
        diag, tiles, lines, sems = refs
    copies = []
    for b in range(blocks):
        at = pl.ds(b * BLK, BLK)
        copies.append(pltpu.make_async_copy(operator.at[at, at], tiles.at[b], sems.at[b]))
        copies[-1].start()
    part_copies = []
    for row in range(owned or 0):
        here = lax.axis_index("rep")
        size = BLK // reps
        start = pl.multiple_of(row * BLK + here * size, size)
        part_copies.append(
            pltpu.make_async_copy(
                coupling.at[pl.ds(start, size)],
                part.at[pl.ds(row * size, size)],
                part_sems.at[row],
            )
        )
        part_copies[-1].start()
    rows = lax.broadcasted_iota(jnp.int32, (BLK, BLK), 0)
    cols = lax.broadcasted_iota(jnp.int32, (BLK, BLK), 1)
    for b in range(blocks):
        step, row = place_of(b, owned, block_index)
        alive = (live_blocks[0, 0] > b).astype(jnp.float32)
        copies[b].wait()
        kept = jnp.where(rows == cols, tiles[b], 0.0)
        slot = step * (owned or 0) + row
        lines[pl.ds(slot, 1), :] = jnp.sum(kept, axis=0, keepdims=True) * alive
    per_step = owned or blocks
    for b in range(blocks):
        d, row = divmod(b, per_step)
        diag[d : d + 1, row * BLK : (row + 1) * BLK] = lines[b : b + 1, :]
    for copy in part_copies:
        copy.wait()


def diagonal(block_index, live_blocks, operator, owned=None, coupling=None):
    blocks = block_index.shape[2]
    per_step = owned or blocks
    reps = lax.axis_size("rep")
    shapes = [jax.ShapeDtypeStruct((blocks // per_step, per_step * BLK), jnp.float32)]
    operands = [pltpu.with_memory_space_constraint(operator, pltpu.HBM)]
    semaphores = [pltpu.SemaphoreType.DMA((blocks,))]
    if owned:
        rows, width = coupling.shape
        shapes.append(jax.ShapeDtypeStruct((rows // reps, width), jnp.float32))
        operands.append(pltpu.with_memory_space_constraint(coupling, pltpu.HBM))
        semaphores.append(pltpu.SemaphoreType.DMA((owned,)))
    return pl.pallas_call(
        functools.partial(diagonal_kernel, blocks, owned, reps),
        out_shape=tuple(shapes),
        in_specs=[SMEM, SMEM] + [ANY] * len(operands),
        out_specs=[VMEM] * len(shapes),
        scratch_shapes=[
            pltpu.VMEM((blocks, BLK, BLK), jnp.float32),
            pltpu.VMEM((blocks, BLK), jnp.float32),
            *semaphores,
        ],
        compiler_params=pltpu.CompilerParams(vmem_limit_bytes=8 << 20),
        cost_estimate=pl.CostEstimate(
            flops=blocks * BLK * BLK, bytes_accessed=4 * blocks * BLK * BLK, transcendentals=0
        ),
        name="diagonal",
    )(block_index, live_blocks, *operands)


def prepare_kernel(blocks, owned, block_index, live_blocks, operator, high, low, rows, sems):
    def fetch(b):
        return pltpu.make_async_copy(operator.at[aligned(b)], rows.at[b], sems.at[b])

    def slot(b):
        step, row = place_of(b, owned, block_index)
        return step * (owned or 0) + row

    for b in range(blocks):
        fetch(b).start()

    def row_block(b, carry):
        target = aligned(slot(b))
        fetch(b).wait()
        for q in range(blocks):
            alive = (live_blocks[0, 0] > b) & (live_blocks[0, 0] > q)
            tile = rows[b, :, q * BLK : (q + 1) * BLK] * alive.astype(jnp.float32)
            across = aligned(slot(q))
            high[target, across], low[target, across] = halves(tile)
        return carry

    lax.fori_loop(0, blocks, row_block, 0)


def prepare(block_index, live_blocks, operator, owned=None):
    blocks = block_index.shape[2]
    size = blocks * BLK
    shape = pltpu.VMEM((size, size), jnp.bfloat16)
    return pl.pallas_call(
        functools.partial(prepare_kernel, blocks, owned),
        out_shape=(shape, shape),
        in_specs=[SMEM, SMEM, ANY],
        out_specs=[VMEM, VMEM],
        scratch_shapes=[
            pltpu.VMEM((blocks, BLK, size), jnp.float32),
            pltpu.SemaphoreType.DMA((blocks,)),
        ],
        compiler_params=pltpu.CompilerParams(vmem_limit_bytes=16 << 20),
        cost_estimate=pl.CostEstimate(
            flops=2 * size * size, bytes_accessed=8 * size * size, transcendentals=0
        ),
        name="prepare",
    )(block_index, live_blocks, pltpu.with_memory_space_constraint(operator, pltpu.HBM))


def assemble_kernel(reps, near, *refs):
    own, parts, (high, low) = refs[0], refs[1:-2], refs[-2:]
    rows = near // BLK
    part_rows = BLK // reps
    high[:near], low[:near] = halves(own[...])
    here = lax.axis_index("rep")
    steps = len(parts) // reps
    for k in range(reps):
        offset = lax.rem(here + k, reps) * part_rows
        for d in range(steps):
            value = parts[k * steps + d]
            for row in range(rows):
                start = (d + 1) * near + row * BLK
                at = pl.ds(pl.multiple_of(start + offset, part_rows), part_rows)
                high[at, :], low[at, :] = halves(value[row * part_rows : (row + 1) * part_rows, :])


def assemble(own, parts, reps):
    near, width = own.shape
    size = near * (len(parts) // reps + 1)
    shape = pltpu.VMEM((size, width), jnp.bfloat16)
    return pl.pallas_call(
        functools.partial(assemble_kernel, reps, near),
        out_shape=(shape, shape),
        in_specs=[VMEM] * (1 + len(parts)),
        out_specs=[VMEM, VMEM],
        compiler_params=pltpu.CompilerParams(vmem_limit_bytes=8 << 20),
        cost_estimate=pl.CostEstimate(
            flops=2 * size * width, bytes_accessed=8 * size * width, transcendentals=0
        ),
        name="assemble",
    )(own, *parts)


def incoming_halves(neighbours, bound_len, responses):
    width = responses[0].shape[1]
    here = lax.axis_index("clus")
    rows = lax.broadcasted_iota(jnp.int32, (1, width), 1)
    incoming = None
    for e in range(len(responses)):
        wanted = lax.rem(here + e, len(responses))
        weight = jnp.zeros((1, width), jnp.float32)
        for j in range(neighbours.shape[1]):
            length = jnp.where(neighbours[0, j] == wanted, bound_len[0, j], 0)
            weight = weight + (rows < length).astype(jnp.float32)
        term = weight * responses[e][...]
        incoming = term if incoming is None else incoming + term
    return jnp.concatenate(halves(incoming), axis=0)


def product_kernel(count, clusters, mode, factor, *refs):
    refs = list(refs)
    high, low, inverse = refs.pop(0), refs.pop(0), refs.pop(0)
    packed = refs.pop()
    if mode in ("corrected", "responding"):
        map_high, map_low = refs.pop(0), refs.pop(0)
    if mode == "corrected":
        neighbours, bound_len = refs.pop(0), refs.pop(0)
        responses = [refs.pop(0) for _ in range(clusters)]
        incoming = incoming_halves(neighbours, bound_len, responses)
        corrected = refs.pop()
    if mode == "responding":
        base = refs.pop(0)
    values, outs = refs[:count], refs[count:]
    columns, near = values[0].shape
    for d in range(count):
        part = values[d][...]
        across = slice(d * near, (d + 1) * near)
        if mode == "scaled":
            part = part * (inverse[d : d + 1, :] * factor)
        if mode == "corrected":
            change = three_products(dot32_t, incoming, map_high[across, :], map_low[across, :])
            part = part + inverse[d : d + 1, :] * change
            if d == 0:
                corrected[...] = part
        packed[:columns, across], packed[columns:, across] = halves(part)
    share = None
    for d in range(count):
        across = slice(d * near, (d + 1) * near)
        total = three_products(dot32, packed[...], high[:, across], low[:, across])
        outs[d][:, :near] = total
        if mode == "responding":
            change = total * (inverse[d : d + 1, :] * -factor)
            if d == 0:
                change = change + base[...]
            change = jnp.concatenate(halves(change), axis=0)
            part = three_products(dot32, change, map_high[across, :], map_low[across, :])
            share = part if share is None else share + part
    if mode == "responding":
        for d in range(count):
            outs[d][:, near:] = share


def product(high, low, inverse, values, mode="plain", factor=1.0, maps=(), extra=()):
    columns, near = values[0].shape
    size = high.shape[0]
    width = near + (maps[0].shape[1] if mode == "responding" else 0)
    shapes = [jax.ShapeDtypeStruct((columns, width), jnp.float32) for _ in values]
    if mode == "corrected":
        shapes.append(jax.ShapeDtypeStruct((columns, near), jnp.float32))
    clusters = len(extra) - 2
    operands = [pinned(high), pinned(low), inverse]
    operands += [pinned(part) for part in maps] + list(extra) + list(values)
    return pl.pallas_call(
        functools.partial(product_kernel, len(values), clusters, mode, factor),
        out_shape=tuple(shapes),
        in_specs=[SMEM if part.dtype == jnp.int32 else VMEM for part in operands],
        out_specs=[VMEM] * len(shapes),
        scratch_shapes=[pltpu.VMEM((2 * columns, size), jnp.bfloat16)],
        compiler_params=pltpu.CompilerParams(vmem_limit_bytes=16 << 20),
        cost_estimate=pl.CostEstimate(
            flops=6 * size * size * columns, bytes_accessed=4 * size * size, transcendentals=0
        ),
        name="product",
    )(*operands)


def finish_kernel(clusters, neighbours, bound_len, inverse, *refs):
    responses, (map_high, map_low, multipliers, out) = refs[:clusters], refs[clusters:]
    incoming = incoming_halves(neighbours, bound_len, responses)
    change = three_products(dot32_t, incoming, map_high[...], map_low[...])
    out[...] = multipliers[...] + inverse[...] * change


def finish(neighbours, bound_len, inverse, responses, maps, multipliers):
    return pl.pallas_call(
        functools.partial(finish_kernel, len(responses)),
        out_shape=jax.ShapeDtypeStruct(multipliers.shape, jnp.float32),
        in_specs=[SMEM] * 2 + [VMEM] * (len(responses) + 4),
        out_specs=VMEM,
        compiler_params=pltpu.CompilerParams(vmem_limit_bytes=8 << 20),
        name="finish",
    )(neighbours, bound_len, inverse, *responses, *maps, multipliers)


def partner(value, axis, step):
    count = lax.axis_size(axis)
    return lax.ppermute(value, axis, [(i, i ^ step) for i in range(count)])


def ahead(value, axis, step):
    count = lax.axis_size(axis)
    return lax.ppermute(value, axis, [((i + step) % count, i) for i in range(count)])


def round_trip(value, axis):
    return [value] + [ahead(value, axis, e) for e in range(1, lax.axis_size(axis))]


def factors():
    sigma = theta / delta
    ratio_prev = 1.0 / sigma
    pairs = []
    for _ in range(CHEB - 1):
        ratio_next = 1.0 / (2.0 * sigma - ratio_prev)
        pairs.append((ratio_next * ratio_prev, 2.0 * ratio_next / delta))
        ratio_prev = ratio_next
    return pairs


def cluster_weights(neighbours, bound_len, width):
    clusters = lax.axis_size("clus")
    here = lax.axis_index("clus")
    row_mask = (lax.iota(jnp.int32, width)[None, :] < bound_len[0][:, None]).astype(jnp.float32)
    rows = []
    for e in range(clusters):
        chosen = (neighbours[0] == (here + e) % clusters).astype(jnp.float32)
        rows.append(jnp.sum(chosen[:, None] * row_mask, axis=0))
    return jnp.stack(rows)


def dense(operator, block_index, live_blocks, loads, coupling, neighbours, bound_len):
    columns, near = loads.shape
    owned = near // BLK
    count = lax.axis_size("sub")
    reps = lax.axis_size("rep")

    def spread(vector):
        return [vector] + [partner(vector, "sub", d) for d in range(1, count)]

    def collect(products):
        arrived = [partner(products[d], "sub", d) for d in range(1, count)]
        return sum(arrived, products[0])

    loads_all = spread(loads)
    diag, own_part = diagonal(block_index, live_blocks, operator, owned, coupling)
    parts = spread(diag)
    rows = [sum(parts[d][d ^ e] for d in range(count)) for e in range(count)]
    inverse_all = 1.0 / jnp.stack(rows)
    inverse = inverse_all[0:1]
    high, low = prepare(block_index, live_blocks, operator, owned)
    fetched = [partner(own_part, "sub", d) for d in range(1, count)]
    maps = None

    residual = loads
    multipliers = jnp.zeros_like(loads)
    corrected = None
    for cycle_index in range(CYCLES):
        if cycle_index > 0:
            *products, multipliers = product(
                high, low, inverse_all, spread(multipliers), "corrected", 1.0, maps, corrected
            )
            residual = loads - collect(products)
        update = inverse * residual / theta
        for sweep_index, (kept, gained) in enumerate(factors()):
            multipliers = multipliers + update
            if sweep_index + 2 < CHEB:
                if cycle_index == 0 and sweep_index == 0:
                    products = product(
                        high, low, inverse_all, loads_all, "scaled", 1.0 / theta
                    )
                else:
                    products = product(high, low, inverse_all, spread(update))
                applied = collect(products)
            else:
                base = multipliers + kept * update + gained * inverse * residual
                products = product(
                    high, low, inverse_all, spread(update), "responding", gained, maps, (base,)
                )
                total = collect(products)
                applied, responses = total[:, :near], total[:, near:]
            residual = residual - applied
            if maps is None:
                *fetched, residual = lax.optimization_barrier((*fetched, residual))
                pieces = list(fetched)
                for k in range(1, reps):
                    pieces += [ahead(part, "rep", k) for part in fetched]
                maps = assemble(coupling, pieces, reps)
            update = kept * update + gained * inverse * residual
        multipliers = multipliers + update
        corrected = (neighbours, bound_len, *round_trip(responses, "clus"))
    near_maps = [part[:near] for part in maps]
    return finish(neighbours, bound_len, inverse, corrected[2:], near_maps, multipliers)


def sparse(operator, block_index, live_blocks, loads, coupling, neighbours, bound_len):
    columns, near = loads.shape
    owned = near // BLK
    blocks = block_index.shape[2]
    subdomains = lax.axis_size("sub")
    total_blocks = owned * subdomains
    (diag,) = diagonal(block_index, live_blocks, operator)
    diag = diag.reshape(blocks, BLK)
    high, low = prepare(block_index, live_blocks, operator)
    ids = block_index[0, 0]
    picker = (ids[:, None] == lax.iota(jnp.int32, total_blocks)[None, :]).astype(jnp.float32)
    diag_term = jnp.dot(picker.T, diag, precision=highest)
    diag_sum = lax.psum_scatter(diag_term, "sub", scatter_dimension=0, tiled=True)
    inverse = 1.0 / diag_sum.reshape(1, near)
    foreign = blocks - owned
    capacity = (foreign + subdomains - 2) // (subdomains - 1)
    total_slots = subdomains * capacity
    far_owner = ids[owned:] // owned
    far_row = ids[owned:] % owned
    positions = lax.iota(jnp.int32, foreign)
    earlier = (
        (far_owner[:, None] == far_owner[None, :]) & (positions[None, :] < positions[:, None])
    ).astype(jnp.int32)
    slot = far_owner * capacity + jnp.sum(earlier, axis=1)
    slot_hit = (slot[:, None] == lax.iota(jnp.int32, total_slots)[None, :]).astype(jnp.int32)
    slot_pick = slot_hit.astype(jnp.float32)
    filled = jnp.sum(slot_hit, axis=0)
    wanted = jnp.where(filled > 0, jnp.sum(slot_hit * far_row[:, None], axis=0), -1)

    def exchange(value):
        shape = value.shape
        value = value.reshape((subdomains, capacity) + shape[1:])
        value = lax.all_to_all(value, "sub", split_axis=0, concat_axis=0, tiled=True)
        return value.reshape(shape)

    asked = exchange(wanted)
    reply_pick = (asked[:, None] == lax.iota(jnp.int32, owned)[None, :]).astype(jnp.float32)

    def pick(table, value):
        return jnp.einsum("pq,qcr->pcr", table, value, precision=highest)

    def by_block(value):
        return jnp.swapaxes(value.reshape(columns, -1, BLK), 0, 1)

    def by_column(value):
        return jnp.swapaxes(value, 0, 1).reshape(columns, -1)

    def apply(vector):
        far = pick(slot_pick, exchange(pick(reply_pick, by_block(vector))))
        gathered = jnp.concatenate([vector, by_column(far)], axis=1)
        (result,) = product(high, low, inverse, [gathered])
        sending = pick(slot_pick.T, by_block(result[:, near:]))
        returned = pick(reply_pick.T, exchange(sending))
        return result[:, :near] + by_column(returned)

    weights = cluster_weights(neighbours, bound_len, coupling.shape[1])
    multipliers = jnp.zeros_like(loads)
    for cycle_index in range(CYCLES):
        residual = loads if cycle_index == 0 else loads - apply(multipliers)
        update = inverse * residual / theta
        for kept, gained in factors():
            multipliers = multipliers + update
            residual = residual - apply(update)
            update = kept * update + gained * inverse * residual
        multipliers = multipliers + update
        responses = lax.psum(jnp.dot(multipliers, coupling, precision=highest), "sub")
        arrived = jnp.stack(round_trip(responses, "clus"))
        incoming = jnp.sum(weights[:, None, :] * arrived, axis=0)
        correction = jnp.einsum("kb,rb->kr", incoming, coupling, precision=highest)
        multipliers = multipliers + inverse * correction
    return multipliers


def local(dual_ops, block_index, live_blocks, loads, coupling, neighbours, bound_len):
    subdomains = lax.axis_size("sub")
    reps = lax.axis_size("rep")
    every_block = block_index.shape[2] * BLK == loads.shape[1] * subdomains
    paired = subdomains & (subdomains - 1) == 0 and BLK % (8 * reps) == 0
    solve = dense if every_block and paired else sparse
    result = solve(
        dual_ops[0, 0], block_index, live_blocks, loads[0].T, coupling[0], neighbours, bound_len
    )
    return result.T[None]


def solution(mesh):
    placed = (
        P(("groups", "clus"), "sub", None, None),
        P(("groups", "clus"), "sub", None),
        P(("groups", "clus"), "sub"),
        P(("groups", "clus"), "sub", "rep"),
        P(("groups", "clus"), "sub", None),
        P(("groups", "clus"), None),
        P(("groups", "clus"), None),
    )
    return jax.shard_map(
        local,
        mesh=mesh,
        in_specs=placed,
        out_specs=P(("groups", "clus"), "sub", "rep"),
        check_vma=False,
    )
```
